32 devices in a mesh: groups: 2 (over y), wide: 4 (over x, core), narrow: 4 (over z).
Axes of the slice: x: 2, y: 2, z: 4, core: 2. Of those that a mesh axis runs over, the one named last changes fastest.
Arguments:
- spectra: bfloat16 [2, 32, 640, 2, 1281], P(None, ('groups', 'wide'), 'narrow'), parts along dimension 1, may hold values from -6 to 6
- legendre: bfloat16 [320, 1281, 128], P('narrow'), may hold values from -0.15625 to 0.15625
- pair_of_slot: int32 [640], replicated, may hold values from 0 to 639, each once
- lat_owner: int32 [128], replicated, may hold values from 0 to 3, as said below
- region_of_lon: int32 [2048], replicated, may hold values from 0 to 63, never falling along the last dimension, each value on 1 to 48 neighbouring positions
Outputs:
- peak: float32 [4, 128, 64], P('groups', 'narrow', 'wide'), parts along dimension 0
- peak_slope: float32 [4, 128, 64], P('groups', 'narrow', 'wide'), parts along dimension 0
The draws below stay inside these ranges and needn't reach their ends.
There are 2 independent parts, one for each index of `groups`. The reference program is written for one: setup_inputs(seed, part) draws one part's arguments, and reference() takes and returns one part's arrays. A program takes and returns all parts, laid end to end along the dimension named above; an argument that names none is the same for every part. Nothing has to cross between parts.
Inputs may be any that keep to these rules, and one draw needn't show every extreme that they name: `lat_owner`: each index of narrow owns exactly 32 latitudes. `region_of_lon`: regions never fall along the longitudes and every region has at least one longitude. `pair_of_slot`: a permutation.
All inputs are finite; a program needn't handle non-finite values.
Results may differ from the reference program's by a relative error of at most 0.0003.
Values sent between devices are 32-bit elements; how exact they have to be, the bound alone decides.
A program may use at most 192 MiB of HBM per device.

```python
import math
import jax
import jax.numpy as jnp
import numpy as np
from jax import lax

M = 1280
LAT = 128
LON = 2048
MEMBERS = 2
PAIRS = 640
PAIR_LEN = 1281
LATH = 64
LAT_DEV = 32
LON_FULL = 5120
TIMES = 16
REGIONS = 64


def draw_lat_owner(key, part):
    shuffled = jax.random.permutation(key, LAT)
    return (shuffled // LAT_DEV).astype(jnp.int32)


def shard_levels(rng, dims, split, least, largest):
    factor_of = 1.0
    for axis_at, parts in split:
        steps = jax.random.uniform(jax.random.fold_in(jax.random.fold_in(rng, 6), axis_at), (parts,), jnp.float32, least / len(split), largest / len(split))
        factor_of = factor_of * jnp.repeat(jnp.exp(steps), dims[axis_at] // parts).reshape((-1,) + (1,) * (len(dims) - 1 - axis_at))
    return factor_of


def split_up(number_of, total, bound, skew):
    loads = [(1 << 20) // math.isqrt(rank ** skew) + 1 for rank in range(2, number_of + 1)]
    surplus, given = total - bound - (number_of - 1), [1] * (number_of - 1)
    while surplus > 0:
        movable = [i for i in range(number_of - 1) if given[i] < bound]
        whole, budget = sum([loads[i] for i in movable]), surplus
        for i in movable:
            extra = min(bound - given[i], max(1, budget * loads[i] // whole), surplus)
            given[i] = given[i] + extra
            surplus = surplus - extra
    return np.array([bound] + given)


def ragged(own_key, number_of, total, most, skew):
    if number_of == 2:
        one = jax.random.randint(own_key, (), max(1, total - most), min(most, total - 1) + 1)
        return jnp.stack([one, total - one])
    tallies = jnp.asarray(split_up(number_of, total, most, skew), jnp.int32)
    twos = (number_of - 1) // 2
    source_of, taker = tallies[1:1 + 2 * twos:2], tallies[2:2 + 2 * twos:2]
    room = jnp.minimum(source_of - 1, most - taker)
    shifted = jax.random.randint(jax.random.fold_in(own_key, 1), (twos,), 0, 1 << 20) % (room + 1)
    tallies = tallies.at[1:1 + 2 * twos:2].set(source_of - shifted).at[2:2 + 2 * twos:2].set(taker + shifted)
    return tallies[jax.random.permutation(jax.random.fold_in(own_key, 2), number_of)]


def scatter_about(key, extent, spread, bound, cuts=(), held_as=jnp.bfloat16):
    drawn = spread * jax.random.normal(key, extent, jnp.float32)
    if cuts:
        drawn = drawn * shard_levels(key, extent, cuts, -0.22, 0.18)
    return jnp.clip(drawn, -bound, bound).astype(held_as)


def setup_inputs(seed: int = 0, part: int = 0) -> dict:
    streams_of = jax.random.split(jax.random.key(seed), 6)
    part_keys = jax.random.split(jax.random.fold_in(streams_of[5], part), 6)
    return {
        "spectra": scatter_about(part_keys[0], (MEMBERS, TIMES, PAIRS, 2, PAIR_LEN), 1.0, 6.0, ((1, 4), (2, 4))),
        "legendre": scatter_about(streams_of[1], (PAIRS // 2, PAIR_LEN, 2 * LATH), M ** -0.5, 0.15625, ((0, 4),)),
        "pair_of_slot": jax.random.permutation(streams_of[2], PAIRS).astype(jnp.int32),
        "lat_owner": draw_lat_owner(jax.random.fold_in(streams_of[5], 71), part),
        "region_of_lon": jnp.searchsorted(jnp.cumsum(ragged(streams_of[4], REGIONS, LON, 48, 0)), jnp.arange(LON), side="right").astype(jnp.int32),
    }


def legendre_slot(coef, table, paired):
    position = jnp.arange(PAIR_LEN, dtype=jnp.int32)
    first_len = M - paired
    leading = position < first_len
    offset = jnp.where(leading, position, position - first_len)
    even_term = offset % 2 == 0
    masks = jnp.stack([leading & even_term, leading & ~even_term, ~leading & even_term, ~leading & ~even_term], axis=0).astype(jnp.float32)
    masked = masks[:, None, None, None, :] * coef.astype(jnp.float32)[None]
    sums = jnp.einsum("getcl,lj->getcj", masked, table.astype(jnp.float32), precision=lax.Precision.HIGHEST)
    north_lead = sums[0] + sums[1]
    south_lead = sums[0] - sums[1]
    north_tail = sums[2] + sums[3]
    south_tail = sums[2] - sums[3]
    lead = jnp.concatenate([north_lead, jnp.flip(south_lead, axis=-1)], axis=-1)
    tail = jnp.concatenate([north_tail, jnp.flip(south_tail, axis=-1)], axis=-1)
    return jnp.stack([lead, tail], axis=0)


def synthesize(operand, waves, start, width):
    columns = start + jnp.arange(width, dtype=jnp.int32)
    phase = (waves[:, None] * columns[None, :]) % LON_FULL
    angle = phase.astype(jnp.float32) * (2.0 * math.pi / LON_FULL)
    cosine = jnp.cos(angle)
    sine = jnp.sin(angle)
    rate = (waves.astype(jnp.float32) / M)[:, None]
    upper = jnp.concatenate([cosine, -rate * sine], axis=1)
    lower = jnp.concatenate([-sine, -rate * cosine], axis=1)
    table = jnp.concatenate([upper, lower], axis=0) * (M ** -0.5)
    return jnp.dot(operand, table, precision=lax.Precision.HIGHEST)


def synthesize_all(operand, waves):
    width = min(512, LON)
    starts = jnp.arange(LON // width, dtype=jnp.int32) * width

    def one_block(begin):
        return synthesize(operand, waves, begin, width)

    blocks = lax.map(one_block, starts)
    blocks = blocks.reshape(blocks.shape[0], blocks.shape[1], 2, width)
    value = jnp.transpose(blocks[:, :, 0], (1, 0, 2)).reshape(operand.shape[0], LON)
    slope = jnp.transpose(blocks[:, :, 1], (1, 0, 2)).reshape(operand.shape[0], LON)
    return value, slope


def region_peak(values, region_of_lon, wanted):
    hits = region_of_lon[:, None] == wanted[None, :]
    masked = jnp.where(hits[None, None], values[..., None], -1e30)
    return masked.max(axis=2)


def reference(spectra, legendre, pair_of_slot, lat_owner, region_of_lon):
    table_all = legendre.reshape(PAIRS // 2, PAIR_LEN, 2, LATH)
    table_all = jnp.transpose(table_all, (0, 2, 1, 3)).reshape(PAIRS, PAIR_LEN, LATH)

    def per_slot(items):
        return legendre_slot(items[0], items[1], items[2])

    slotted = lax.map(per_slot, (jnp.moveaxis(spectra, 2, 0), table_all, pair_of_slot))
    grid = jnp.zeros((M, MEMBERS, TIMES, 2, LAT), jnp.float32)
    grid = grid.at[pair_of_slot].set(slotted[:, 0])
    grid = grid.at[M - 1 - pair_of_slot].set(slotted[:, 1])
    order = jnp.argsort(lat_owner, stable=True).astype(jnp.int32)
    grid = jnp.take(grid, order, axis=4)
    operand = jnp.transpose(grid, (1, 2, 4, 3, 0)).reshape(MEMBERS * TIMES * LAT, 2 * M)
    waves = jnp.arange(M, dtype=jnp.int32)
    value, slope = synthesize_all(operand, waves)
    value = value.reshape(MEMBERS, TIMES, LAT, LON).max(axis=1)
    slope = jnp.abs(slope).reshape(MEMBERS, TIMES, LAT, LON).max(axis=1)
    wanted = jnp.arange(REGIONS, dtype=jnp.int32)
    peak = region_peak(value, region_of_lon, wanted)
    peak_slope = region_peak(slope, region_of_lon, wanted)
    return peak, peak_slope
```

```python
import functools
import math

import jax
import jax.numpy as jnp
from jax import lax
from jax.experimental import pallas as pl
from jax.experimental.pallas import tpu as pltpu
from jax.sharding import PartitionSpec as P

M = 1280
LON = 2048
REG_DEV = 16
LON_FULL = 5120


def synthesize(operand, waves, start, width):
    columns = start + jnp.arange(width, dtype=jnp.int32)
    phase = waves[:, None] * columns[None, :] % LON_FULL
    angle = phase.astype(jnp.float32) * (2.0 * math.pi / LON_FULL)
    cosine = jnp.cos(angle)
    sine = jnp.sin(angle)
    rate = (waves.astype(jnp.float32) / M)[:, None]
    upper = jnp.concatenate([cosine, -rate * sine], axis=1)
    lower = jnp.concatenate([-sine, -rate * cosine], axis=1)
    table = jnp.concatenate([upper, lower], axis=0) * M ** (-0.5)
    return jnp.dot(operand, table, precision=lax.Precision.HIGHEST)


def synthesize_all(operand, waves):
    width = min(512, LON)
    starts = jnp.arange(LON // width, dtype=jnp.int32) * width

    def one_block(begin):
        return synthesize(operand, waves, begin, width)

    blocks = lax.map(one_block, starts)
    blocks = blocks.reshape(blocks.shape[0], blocks.shape[1], 2, width)
    value = jnp.transpose(blocks[:, :, 0], (1, 0, 2)).reshape(operand.shape[0], LON)
    slope = jnp.transpose(blocks[:, :, 1], (1, 0, 2)).reshape(operand.shape[0], LON)
    return (value, slope)


def region_peak(values, region_of_lon, wanted):
    hits = region_of_lon[:, None] == wanted[None, :]
    masked = jnp.where(hits[None, None], values[..., None], -1e30)
    return masked.max(axis=2)


def per_device_plain(spectra, legendre, pair_of_slot, lat_owner, region_of_lon):
    members = spectra.shape[0]
    steps_here = spectra.shape[1]
    slot_count = spectra.shape[2]
    length = spectra.shape[4]
    half_count = legendre.shape[0]
    lat_half = legendre.shape[2] // 2
    here = lax.axis_index("narrow")
    paired = lax.dynamic_slice_in_dim(pair_of_slot, here * slot_count, slot_count)
    position = jnp.arange(length, dtype=jnp.int32)[None, :]
    first_len = (M - paired)[:, None]
    leading = position < first_len
    offset = jnp.where(leading, position, position - first_len)
    even_term = offset % 2 == 0
    masks = jnp.stack(
        [leading & even_term, leading & ~even_term, ~leading & even_term, ~leading & ~even_term],
        axis=1,
    ).astype(jnp.bfloat16)
    ordered = jnp.transpose(spectra, (2, 0, 1, 3, 4))
    masked = masks[:, :, None, None, None, :] * ordered[:, None]
    masked = masked.reshape(half_count, 2, -1, length)
    table = legendre.reshape(half_count, length, 2, lat_half)
    sums = jnp.einsum("abrl,albj->abrj", masked, table, preferred_element_type=jnp.float32)
    sums = sums.reshape(slot_count, 4, members, steps_here, 2, lat_half)
    north_lead = sums[:, 0] + sums[:, 1]
    south_lead = sums[:, 0] - sums[:, 1]
    north_tail = sums[:, 2] + sums[:, 3]
    south_tail = sums[:, 2] - sums[:, 3]
    lead = jnp.concatenate([north_lead, jnp.flip(south_lead, axis=-1)], axis=-1)
    tail = jnp.concatenate([north_tail, jnp.flip(south_tail, axis=-1)], axis=-1)
    waved = jnp.stack([lead, tail], axis=1).reshape(2 * slot_count, members, steps_here, 2, -1)
    order = jnp.argsort(lat_owner, stable=True)
    waved = jnp.take(waved, order, axis=4)
    arrived = lax.all_to_all(waved, "narrow", split_axis=4, concat_axis=0, tiled=True)
    waves = jnp.stack([pair_of_slot, M - 1 - pair_of_slot], axis=1).reshape(-1)
    lat_here = arrived.shape[4]
    operand = jnp.transpose(arrived, (1, 2, 4, 3, 0)).reshape(members * steps_here * lat_here, -1)
    value, slope = synthesize_all(operand, waves)
    value = value.reshape(members, steps_here, lat_here, LON).max(axis=1)
    slope = jnp.abs(slope).reshape(members, steps_here, lat_here, LON).max(axis=1)
    wide_count = lax.axis_size("wide")
    mine_start = lax.axis_index("wide") * REG_DEV
    wanted = jnp.arange(REG_DEV * wide_count, dtype=jnp.int32)
    peaks = region_peak(value, region_of_lon, wanted)
    slopes = region_peak(slope, region_of_lon, wanted)
    peaks, slopes = lax.pmax((peaks, slopes), "wide")
    peak = lax.dynamic_slice_in_dim(peaks, mine_start, REG_DEV, 2)
    peak_slope = lax.dynamic_slice_in_dim(slopes, mine_start, REG_DEV, 2)
    return (peak, peak_slope)


CHUNK = 16
KCHUNKS = 2
FINE = 32
WINDOW = 56
MESH = pl.DeviceIdType.MESH


def greet(axis, count):
    me = lax.axis_index(axis)
    barrier = pltpu.get_barrier_semaphore()
    for step in range(1, count):
        pl.semaphore_signal(barrier, inc=1, device_id={axis: lax.rem(me + step, count)}, device_id_type=MESH)
    pl.semaphore_wait(barrier, count - 1)


def split(values):
    high = values.astype(jnp.bfloat16)
    low = (values - high.astype(jnp.float32)).astype(jnp.bfloat16)
    return high, low


def dot(left, right):
    return jnp.dot(left, right, preferred_element_type=jnp.float32)


def fields_kernel(
    dims, first_ref, x_ref, table_ref, place_ref, turn_ref, coarse_ref, fine_ref, out_ref,
    sums, sent, held, part_cos, part_sin, send_sem, recv_sem,
):
    narrow, chunks, rows, members, steps_here, lat_here = dims
    step = pl.program_id(0)
    me = lax.axis_index("narrow")
    lanes = members * 2 * 128

    def copy_to(chunk, ahead):
        target = lax.rem(me + ahead, narrow)
        return pltpu.make_async_remote_copy(
            src_ref=sent.at[chunk, target], dst_ref=held.at[chunk, me],
            send_sem=send_sem.at[chunk, target], recv_sem=recv_sem.at[chunk, me],
            device_id={"narrow": target}, device_id_type=MESH,
        )

    def copy_from(chunk, ahead):
        origin = lax.rem(me + ahead, narrow)
        return pltpu.make_async_remote_copy(
            src_ref=sent.at[chunk, origin], dst_ref=held.at[chunk, origin],
            send_sem=send_sem.at[chunk, origin], recv_sem=recv_sem.at[chunk, origin],
            device_id={"narrow": origin}, device_id_type=MESH,
        )

    @pl.when(step == 0)
    def _():
        greet("narrow", narrow)

    @pl.when((step >= 1) & (step <= chunks))
    def _():
        for ahead in (2, 1, 3) if narrow == 4 else range(1, narrow):
            copy_to(step - 1, ahead).start()

    @pl.when(step < chunks)
    def _():
        position = lax.broadcasted_iota(jnp.int32, (1, M), 1)
        lane = lax.broadcasted_iota(jnp.int32, (rows, 128), 1)

        def one_pair(at, carry):
            parts = []
            extras = []
            for half in range(2):
                slot = 2 * at + half
                first_len = M - first_ref[step * CHUNK + slot]
                leading = (position < first_len).astype(jnp.float32)
                trailing = 1.0 - leading
                sign_lead = (1 - 2 * (position & 1)).astype(jnp.float32)
                flip = (1 - 2 * (first_len & 1)).astype(jnp.float32)
                x = x_ref[slot]
                body = x[:, :M]
                for mask in (leading, leading * sign_lead, trailing, trailing * (sign_lead * flip)):
                    parts.append(body * mask.astype(jnp.bfloat16))
                last = x[:, M:].astype(jnp.float32)
                extras.append((last, flip))
            table = table_ref[at]
            out = dot(jnp.concatenate(parts, axis=0), table[:M])
            edge = table[M:].astype(jnp.float32)
            for half in range(2):
                base = half * 4 * rows
                piece = [out[base + v * rows:base + (v + 1) * rows] for v in range(4)]
                last, flip = extras[half]
                term = last * edge
                piece[2] = piece[2] + term
                piece[3] = piece[3] + term * flip
                for tail_at in range(2):
                    north, south = piece[2 * tail_at], piece[2 * tail_at + 1]
                    if half == 0:
                        both = jnp.where(lane < 64, north, pltpu.roll(south, 64, 1))
                    else:
                        both = jnp.where(lane < 64, pltpu.roll(north, 64, 1), south)
                    at_row = (tail_at * CHUNK + 2 * at + half) * rows
                    sums[pl.ds(pl.multiple_of(at_row, rows), rows), :] = both
            return carry

        lax.fori_loop(0, CHUNK // 2, one_pair, 0)
        for c in range(2):
            for e in range(members):
                wide_rows = jnp.concatenate(
                    [sums[pl.ds((e * steps_here + t) * 2 + c, 2 * CHUNK, stride=rows), :] for t in range(steps_here)],
                    axis=1,
                )
                high, low = split(wide_rows)
                moved = dot(high, place_ref[...]) + dot(low, place_ref[...])
                begin = (c * members + e) * 128
                for d in range(narrow):
                    sent[step, d, :, begin:begin + 128] = moved[:, d * 128:(d + 1) * 128]
        held[step, me] = sent[step, me]

    @pl.when(step >= chunks)
    def _():
        at = step - chunks
        half = members * 128
        for k in range(KCHUNKS):
            for ahead in range(1, narrow):
                copy_from(at * KCHUNKS + k, ahead).wait_recv()
        depth = KCHUNKS * narrow * 2 * CHUNK
        data = jnp.concatenate(
            [held[at * KCHUNKS + k, d] for k in range(KCHUNKS) for d in range(narrow)], axis=0
        )
        real, imag = data[:, :half], data[:, half:]
        turn = turn_ref[...]
        cos0, sin0, rate = turn[:, 0:1], turn[:, 1:2], turn[:, 2:3]
        a = real * cos0 - imag * sin0
        b = real * sin0 + imag * cos0
        even_hi, even_lo = split(jnp.concatenate([a, -rate * b], axis=1))
        odd_hi, odd_lo = split(jnp.concatenate([b, rate * a], axis=1))
        group = 8
        tall = group * FINE

        def one_group(g, carry):
            cosines, sines = [], []
            c2, s2 = fine_ref[0], fine_ref[1]
            cu = coarse_ref[0, pl.ds(pl.multiple_of(g * group, group), group), :]
            su = coarse_ref[1, pl.ds(pl.multiple_of(g * group, group), group), :]
            for u in range(group):
                c1, s1 = cu[u:u + 1], su[u:u + 1]
                cosines.append(c1 * c2 - s1 * s2)
                sines.append(s1 * c2 + c1 * s2)
            cos_hi, cos_lo = split(jnp.concatenate(cosines, axis=0))
            sin_hi, sin_lo = split(jnp.concatenate(sines, axis=0))
            where_to = pl.ds(pl.multiple_of(g * tall, tall), tall)
            new_cos = dot(cos_hi, even_hi) + dot(cos_lo, even_hi) + dot(cos_hi, even_lo)
            new_sin = dot(sin_hi, odd_hi) + dot(sin_lo, odd_hi) + dot(sin_hi, odd_lo)

            @pl.when(at == 0)
            def _():
                part_cos[where_to, :] = new_cos
                part_sin[where_to, :] = new_sin

            @pl.when(at > 0)
            def _():
                part_cos[where_to, :] += new_cos
                part_sin[where_to, :] += new_sin

            return carry

        lax.fori_loop(0, part_cos.shape[0] // tall, one_group, 0)

    @pl.when(step == pl.num_programs(0) - 1)
    def _():
        tall = 64
        owner = lax.broadcasted_iota(jnp.int32, (tall, 128), 1) // lat_here

        def fold(g, carry):
            where_from = pl.ds(pl.multiple_of(g * tall, tall), tall)
            even, odd = part_cos[where_from, :], part_sin[where_from, :]
            for side, full in enumerate((even + odd, even - odd)):
                chosen = None
                for n in range(2 * members):
                    piece = full[:, n * 128:(n + 1) * 128]
                    if n >= members:
                        piece = jnp.abs(piece)
                    reach = lat_here
                    while reach < 128:
                        piece = jnp.maximum(piece, pltpu.roll(piece, reach, 1))
                        reach *= 2
                    chosen = piece if chosen is None else jnp.where(owner == n, piece, chosen)
                out_ref[side, where_from, :] = chosen
            return carry

        lax.fori_loop(0, part_cos.shape[0] // tall, fold, 0)

        def drain(chunk, carry):
            for ahead in range(1, narrow):
                copy_to(chunk, ahead).wait_send()
            return carry

        lax.fori_loop(0, chunks, drain, 0)


def region_kernel(regions, edge_ref, field_ref, out_ref):
    half = field_ref.shape[1]
    row = lax.broadcasted_iota(jnp.int32, (WINDOW, 128), 0)

    def one_region(r, carry):
        begin, end = edge_ref[r], edge_ref[r + 1]
        best = jnp.full((1, 128), -1e30, jnp.float32)
        for side in range(2):
            low = half - end if side == 0 else begin - half
            high = half - begin if side == 0 else end - half
            at = jnp.clip(low // 8 * 8, 0, half - WINDOW)
            at = pl.multiple_of(at, 8)
            data = field_ref[side, pl.ds(at, WINDOW), :]
            here = (row >= low - at) & (row < high - at)
            best = jnp.maximum(best, jnp.max(jnp.where(here, data, -1e30), axis=0, keepdims=True))
        out_ref[pl.ds(r, 1), :] = best
        return carry

    lax.fori_loop(0, regions, one_region, 0)


def wide_kernel(wide, mine_ref, out_ref, held, send_sem, recv_sem):
    me = lax.axis_index("wide")
    count = out_ref.shape[0]
    greet("wide", wide)

    def copy(ahead, arriving):
        other = lax.rem(me + ahead, wide)
        return pltpu.make_async_remote_copy(
            src_ref=mine_ref.at[other], dst_ref=held.at[other if arriving else me],
            send_sem=send_sem.at[other], recv_sem=recv_sem.at[other if arriving else me],
            device_id={"wide": other}, device_id_type=MESH,
        )

    for ahead in range(1, wide):
        copy(ahead, False).start()
    best = mine_ref[me]
    for ahead in range(1, wide):
        copy(ahead, True).wait_recv()
        best = jnp.maximum(best, held[lax.rem(me + ahead, wide)])
    out_ref[...] = best
    for ahead in range(1, wide):
        copy(ahead, False).wait_send()


def per_device(spectra, legendre, pair_of_slot, lat_owner, region_of_lon):
    members, steps_here, slot_count, _, length = spectra.shape
    half_count = legendre.shape[0]
    lat = legendre.shape[2]
    narrow, wide = lax.axis_size("narrow"), lax.axis_size("wide")
    lat_here = lat // narrow
    lon = region_of_lon.shape[0]
    half_lon = lon // 2
    rows = members * steps_here * 2
    chunks = slot_count // CHUNK
    here = lax.axis_index("narrow")
    paired = lax.dynamic_slice_in_dim(pair_of_slot, here * slot_count, slot_count)
    x = jnp.transpose(spectra, (2, 0, 1, 3, 4)).reshape(slot_count, rows, length)

    ids = jnp.arange(lat, dtype=jnp.int32)
    before = (lat_owner[:, None] < lat_owner[None, :]) | (
        (lat_owner[:, None] == lat_owner[None, :]) & (ids[:, None] < ids[None, :])
    )
    rank = jnp.sum(before.astype(jnp.int32), axis=0)
    rank = jnp.concatenate([rank[:lat // 2], jnp.flip(rank[lat // 2:])])
    target = (rank // lat_here)[None, :] * 128 + jnp.arange(steps_here)[:, None] * lat_here + (rank % lat_here)[None, :]
    place = (target.reshape(-1)[:, None] == jnp.arange(narrow * 128)[None, :]).astype(jnp.bfloat16)

    lead = jnp.transpose(pair_of_slot.reshape(narrow, chunks, CHUNK), (1, 0, 2))
    waves = jnp.stack([lead, M - 1 - lead], axis=2).reshape(-1)
    unit = 2.0 * math.pi / (2 * LON_FULL)

    def angle(factor):
        return ((waves * factor) % (2 * LON_FULL)).astype(jnp.float32) * unit

    start = angle(lon - 1)
    scale = M ** -0.5
    turn = jnp.stack(
        [jnp.cos(start) * scale, jnp.sin(start) * scale, waves.astype(jnp.float32) / M, jnp.zeros_like(start)], axis=1
    )
    coarse = angle((jnp.arange(half_lon // FINE, dtype=jnp.int32) * (2 * FINE))[:, None])
    fine = angle((jnp.arange(FINE, dtype=jnp.int32) * 2 + 1)[:, None])
    coarse = jnp.stack([jnp.cos(coarse), jnp.sin(coarse)])
    fine = jnp.stack([jnp.cos(fine), jnp.sin(fine)])

    dims = (narrow, chunks, rows, members, steps_here, lat_here)
    depth = KCHUNKS * narrow * 2 * CHUNK
    lanes = 2 * members * 128
    tail = chunks // KCHUNKS

    def first(i, *_):
        return jnp.minimum(i, chunks - 1)

    def later(i, *_):
        return jnp.maximum(i - chunks, 0)

    fields = pl.pallas_call(
        functools.partial(fields_kernel, dims),
        grid=(chunks + tail,),
        in_specs=[
            pl.BlockSpec(memory_space=pltpu.SMEM),
            pl.BlockSpec((CHUNK, rows, length), lambda i: (first(i), 0, 0)),
            pl.BlockSpec((CHUNK // 2, length, lat), lambda i: (first(i), 0, 0)),
            pl.BlockSpec(place.shape, lambda i: (0, 0)),
            pl.BlockSpec((depth, turn.shape[1]), lambda i: (later(i), 0)),
            pl.BlockSpec((2, half_lon // FINE, depth), lambda i: (0, 0, later(i))),
            pl.BlockSpec((2, FINE, depth), lambda i: (0, 0, later(i))),
        ],
        out_specs=pl.BlockSpec((2, half_lon, 128), lambda i: (0, 0, 0)),
        out_shape=jax.ShapeDtypeStruct((2, half_lon, 128), jnp.float32),
        scratch_shapes=[
            pltpu.VMEM((2 * CHUNK * rows, 128), jnp.float32),
            pltpu.VMEM((chunks, narrow, 2 * CHUNK, lanes), jnp.float32),
            pltpu.VMEM((chunks, narrow, 2 * CHUNK, lanes), jnp.float32),
            pltpu.VMEM((half_lon, lanes), jnp.float32),
            pltpu.VMEM((half_lon, lanes), jnp.float32),
            pltpu.SemaphoreType.DMA((chunks, narrow)),
            pltpu.SemaphoreType.DMA((chunks, narrow)),
        ],
        compiler_params=pltpu.CompilerParams(
            collective_id=0, has_side_effects=True, vmem_limit_bytes=56 * 1024 * 1024,
            dimension_semantics=("arbitrary",),
        ),
    )(paired, x, legendre, place, turn, coarse, fine)

    regions = REG_DEV * wide
    edges = jnp.sum(
        (region_of_lon[None, :] < jnp.arange(regions + 1, dtype=jnp.int32)[:, None]).astype(jnp.int32), axis=1
    )
    peaks = pl.pallas_call(
        functools.partial(region_kernel, regions),
        in_specs=[pl.BlockSpec(memory_space=pltpu.SMEM), pl.BlockSpec(memory_space=pltpu.VMEM)],
        out_specs=pl.BlockSpec(memory_space=pltpu.VMEM),
        out_shape=jax.ShapeDtypeStruct((regions, 128), jnp.float32),
    )(edges, fields)
    best = pl.pallas_call(
        functools.partial(wide_kernel, wide),
        in_specs=[pl.BlockSpec(memory_space=pltpu.VMEM)],
        out_specs=pl.BlockSpec(memory_space=pltpu.VMEM),
        out_shape=jax.ShapeDtypeStruct((REG_DEV, 128), jnp.float32),
        scratch_shapes=[
            pltpu.VMEM((wide, REG_DEV, 128), jnp.float32),
            pltpu.SemaphoreType.DMA((wide,)),
            pltpu.SemaphoreType.DMA((wide,)),
        ],
        compiler_params=pltpu.CompilerParams(collective_id=1, has_side_effects=True),
    )(peaks.reshape(wide, REG_DEV, 128))
    best = jnp.transpose(best.reshape(REG_DEV, 2, members, lat_here), (1, 2, 3, 0))
    return (best[0], best[1])


def solution(mesh):
    in_specs = (
        P(None, ("groups", "wide"), "narrow", None, None),
        P("narrow", None, None),
        P(),
        P(),
        P(),
    )
    out_specs = (P("groups", "narrow", "wide"), P("groups", "narrow", "wide"))

    def body(spectra, legendre, *rest):
        members, steps_here, slot_count = spectra.shape[:3]
        lat_here = legendre.shape[2] // mesh.shape["narrow"]
        packs = steps_here * lat_here == 128 and 2 * members * lat_here == 128
        packs = packs and slot_count % (CHUNK * KCHUNKS) == 0 and legendre.shape[2] == 128
        chosen = per_device if packs else per_device_plain
        return chosen(spectra, legendre, *rest)

    return jax.shard_map(
        body, mesh=mesh, in_specs=in_specs, out_specs=out_specs, check_vma=False
    )
```

```python
import functools
import math

import jax
import jax.numpy as jnp
from jax import lax
from jax.experimental import pallas as pl
from jax.experimental.pallas import tpu as pltpu
from jax.sharding import PartitionSpec as P

M = 1280
LON = 2048
REG_DEV = 16
LON_FULL = 5120


def synthesize(operand, waves, start, width):
    columns = start + jnp.arange(width, dtype=jnp.int32)
    phase = waves[:, None] * columns[None, :] % LON_FULL
    angle = phase.astype(jnp.float32) * (2.0 * math.pi / LON_FULL)
    cosine = jnp.cos(angle)
    sine = jnp.sin(angle)
    rate = (waves.astype(jnp.float32) / M)[:, None]
    upper = jnp.concatenate([cosine, -rate * sine], axis=1)
    lower = jnp.concatenate([-sine, -rate * cosine], axis=1)
    table = jnp.concatenate([upper, lower], axis=0) * M ** (-0.5)
    return jnp.dot(operand, table, precision=lax.Precision.HIGHEST)


def synthesize_all(operand, waves):
    width = min(512, LON)
    starts = jnp.arange(LON // width, dtype=jnp.int32) * width

    def one_block(begin):
        return synthesize(operand, waves, begin, width)

    blocks = lax.map(one_block, starts)
    blocks = blocks.reshape(blocks.shape[0], blocks.shape[1], 2, width)
    value = jnp.transpose(blocks[:, :, 0], (1, 0, 2)).reshape(operand.shape[0], LON)
    slope = jnp.transpose(blocks[:, :, 1], (1, 0, 2)).reshape(operand.shape[0], LON)
    return (value, slope)


def region_peak(values, region_of_lon, wanted):
    hits = region_of_lon[:, None] == wanted[None, :]
    masked = jnp.where(hits[None, None], values[..., None], -1e30)
    return masked.max(axis=2)


def per_device_plain(spectra, legendre, pair_of_slot, lat_owner, region_of_lon):
    members = spectra.shape[0]
    steps_here = spectra.shape[1]
    slot_count = spectra.shape[2]
    length = spectra.shape[4]
    half_count = legendre.shape[0]
    lat_half = legendre.shape[2] // 2
    here = lax.axis_index("narrow")
    paired = lax.dynamic_slice_in_dim(pair_of_slot, here * slot_count, slot_count)
    position = jnp.arange(length, dtype=jnp.int32)[None, :]
    first_len = (M - paired)[:, None]
    leading = position < first_len
    offset = jnp.where(leading, position, position - first_len)
    even_term = offset % 2 == 0
    masks = jnp.stack(
        [leading & even_term, leading & ~even_term, ~leading & even_term, ~leading & ~even_term],
        axis=1,
    ).astype(jnp.bfloat16)
    ordered = jnp.transpose(spectra, (2, 0, 1, 3, 4))
    masked = masks[:, :, None, None, None, :] * ordered[:, None]
    masked = masked.reshape(half_count, 2, -1, length)
    table = legendre.reshape(half_count, length, 2, lat_half)
    sums = jnp.einsum("abrl,albj->abrj", masked, table, preferred_element_type=jnp.float32)
    sums = sums.reshape(slot_count, 4, members, steps_here, 2, lat_half)
    north_lead = sums[:, 0] + sums[:, 1]
    south_lead = sums[:, 0] - sums[:, 1]
    north_tail = sums[:, 2] + sums[:, 3]
    south_tail = sums[:, 2] - sums[:, 3]
    lead = jnp.concatenate([north_lead, jnp.flip(south_lead, axis=-1)], axis=-1)
    tail = jnp.concatenate([north_tail, jnp.flip(south_tail, axis=-1)], axis=-1)
    waved = jnp.stack([lead, tail], axis=1).reshape(2 * slot_count, members, steps_here, 2, -1)
    order = jnp.argsort(lat_owner, stable=True)
    waved = jnp.take(waved, order, axis=4)
    arrived = lax.all_to_all(waved, "narrow", split_axis=4, concat_axis=0, tiled=True)
    waves = jnp.stack([pair_of_slot, M - 1 - pair_of_slot], axis=1).reshape(-1)
    lat_here = arrived.shape[4]
    operand = jnp.transpose(arrived, (1, 2, 4, 3, 0)).reshape(members * steps_here * lat_here, -1)
    value, slope = synthesize_all(operand, waves)
    value = value.reshape(members, steps_here, lat_here, LON).max(axis=1)
    slope = jnp.abs(slope).reshape(members, steps_here, lat_here, LON).max(axis=1)
    wide_count = lax.axis_size("wide")
    mine_start = lax.axis_index("wide") * REG_DEV
    wanted = jnp.arange(REG_DEV * wide_count, dtype=jnp.int32)
    peaks = region_peak(value, region_of_lon, wanted)
    slopes = region_peak(slope, region_of_lon, wanted)
    peaks, slopes = lax.pmax((peaks, slopes), "wide")
    peak = lax.dynamic_slice_in_dim(peaks, mine_start, REG_DEV, 2)
    peak_slope = lax.dynamic_slice_in_dim(slopes, mine_start, REG_DEV, 2)
    return (peak, peak_slope)


CHUNK = 16
KCHUNKS = 2
FINE = 32
WINDOW = 56
MESH = pl.DeviceIdType.MESH


def greet(axis, count):
    me = lax.axis_index(axis)
    barrier = pltpu.get_barrier_semaphore()
    for step in range(1, count):
        pl.semaphore_signal(barrier, inc=1, device_id={axis: lax.rem(me + step, count)}, device_id_type=MESH)
    pl.semaphore_wait(barrier, count - 1)


def split(values):
    high = values.astype(jnp.bfloat16)
    low = (values - high.astype(jnp.float32)).astype(jnp.bfloat16)
    return high, low


def dot(left, right):
    return jnp.dot(left, right, preferred_element_type=jnp.float32)


def fields_kernel(
    dims, first_ref, x_ref, table_ref, place_ref, turn_ref, coarse_ref, fine_ref, out_ref,
    lined, spread, sums, sent, held, part_cos, part_sin, send_sem, recv_sem,
):
    narrow, chunks, rows, members, steps_here, lat_here = dims
    step = pl.program_id(0)
    me = lax.axis_index("narrow")
    lanes = members * 2 * 128

    def copy_to(chunk, ahead):
        target = lax.rem(me + ahead, narrow)
        return pltpu.make_async_remote_copy(
            src_ref=sent.at[chunk, target], dst_ref=held.at[chunk, me],
            send_sem=send_sem.at[chunk, target], recv_sem=recv_sem.at[chunk, me],
            device_id={"narrow": target}, device_id_type=MESH,
        )

    def copy_from(chunk, ahead):
        origin = lax.rem(me + ahead, narrow)
        return pltpu.make_async_remote_copy(
            src_ref=sent.at[chunk, origin], dst_ref=held.at[chunk, origin],
            send_sem=send_sem.at[chunk, origin], recv_sem=recv_sem.at[chunk, origin],
            device_id={"narrow": origin}, device_id_type=MESH,
        )

    @pl.when(step == 0)
    def _():
        greet("narrow", narrow)

    @pl.when((step >= 1) & (step <= chunks))
    def _():
        for ahead in (2, 1, 3) if narrow == 4 else range(1, narrow):
            copy_to(step - 1, ahead).start()

    @pl.when(step < chunks)
    def _():
        position = lax.broadcasted_iota(jnp.int32, (1, M), 1)
        lane = lax.broadcasted_iota(jnp.int32, (rows, 128), 1)
        pairs = CHUNK // 2
        block = M // 8

        def widen(n, carry):
            part = table_ref[pl.ds(n * block, block)].astype(jnp.float32)
            where_to = pl.ds(pl.multiple_of(n * block * pairs, 8), block * pairs)
            spread[where_to, :] = part.reshape(block * pairs, 128)
            return carry

        lax.fori_loop(0, 8, widen, 0)
        spread[M * pairs:, :] = table_ref[M].astype(jnp.float32)

        def one_pair(at, carry):
            parts = []
            extras = []
            for half in range(2):
                slot = 2 * at + half
                first_len = M - first_ref[step * CHUNK + slot]
                leading = (position < first_len).astype(jnp.float32)
                trailing = 1.0 - leading
                sign_lead = (1 - 2 * (position & 1)).astype(jnp.float32)
                flip = (1 - 2 * (first_len & 1)).astype(jnp.float32)
                for e in range(members):
                    for t in range(steps_here):
                        row = 2 * (e * steps_here + t)
                        lined[half, row:row + 2, :] = x_ref[e, t, slot].astype(jnp.float32)
                body = lined[half, :, :M].astype(jnp.bfloat16)
                for mask in (leading, leading * sign_lead, trailing, trailing * (sign_lead * flip)):
                    parts.append(body * mask.astype(jnp.bfloat16))
                last = lined[half, :, M:]
                extras.append((last, flip))
            table = spread[pl.ds(at, M, stride=pairs), :].astype(jnp.bfloat16)
            out = dot(jnp.concatenate(parts, axis=0), table)
            edge = spread[pl.ds(M * pairs + at, 1), :]
            for half in range(2):
                base = half * 4 * rows
                piece = [out[base + v * rows:base + (v + 1) * rows] for v in range(4)]
                last, flip = extras[half]
                term = last * edge
                piece[2] = piece[2] + term
                piece[3] = piece[3] + term * flip
                for tail_at in range(2):
                    north, south = piece[2 * tail_at], piece[2 * tail_at + 1]
                    if half == 0:
                        both = jnp.where(lane < 64, north, pltpu.roll(south, 64, 1))
                    else:
                        both = jnp.where(lane < 64, pltpu.roll(north, 64, 1), south)
                    at_row = (tail_at * CHUNK + 2 * at + half) * rows
                    sums[pl.ds(pl.multiple_of(at_row, rows), rows), :] = both
            return carry

        lax.fori_loop(0, CHUNK // 2, one_pair, 0)
        for c in range(2):
            for e in range(members):
                wide_rows = jnp.concatenate(
                    [sums[pl.ds((e * steps_here + t) * 2 + c, 2 * CHUNK, stride=rows), :] for t in range(steps_here)],
                    axis=1,
                )
                high, low = split(wide_rows)
                moved = dot(high, place_ref[...]) + dot(low, place_ref[...])
                begin = (c * members + e) * 128
                for d in range(narrow):
                    sent[step, d, :, begin:begin + 128] = moved[:, d * 128:(d + 1) * 128]
        held[step, me] = sent[step, me]

    @pl.when(step >= chunks)
    def _():
        at = step - chunks
        half = members * 128
        for k in range(KCHUNKS):
            for ahead in range(1, narrow):
                copy_from(at * KCHUNKS + k, ahead).wait_recv()
        depth = KCHUNKS * narrow * 2 * CHUNK
        data = jnp.concatenate(
            [held[at * KCHUNKS + k, d] for k in range(KCHUNKS) for d in range(narrow)], axis=0
        )
        real, imag = data[:, :half], data[:, half:]
        turn = turn_ref[...]
        cos0, sin0, rate = turn[:, 0:1], turn[:, 1:2], turn[:, 2:3]
        a = real * cos0 - imag * sin0
        b = real * sin0 + imag * cos0
        even_hi, even_lo = split(jnp.concatenate([a, -rate * b], axis=1))
        odd_hi, odd_lo = split(jnp.concatenate([b, rate * a], axis=1))
        group = 8
        tall = group * FINE

        def one_group(g, carry):
            cosines, sines = [], []
            c2, s2 = fine_ref[0], fine_ref[1]
            cu = coarse_ref[0, pl.ds(pl.multiple_of(g * group, group), group), :]
            su = coarse_ref[1, pl.ds(pl.multiple_of(g * group, group), group), :]
            for u in range(group):
                c1, s1 = cu[u:u + 1], su[u:u + 1]
                cosines.append(c1 * c2 - s1 * s2)
                sines.append(s1 * c2 + c1 * s2)
            cos_hi, cos_lo = split(jnp.concatenate(cosines, axis=0))
            sin_hi, sin_lo = split(jnp.concatenate(sines, axis=0))
            where_to = pl.ds(pl.multiple_of(g * tall, tall), tall)
            new_cos = dot(cos_hi, even_hi) + dot(cos_lo, even_hi) + dot(cos_hi, even_lo)
            new_sin = dot(sin_hi, odd_hi) + dot(sin_lo, odd_hi) + dot(sin_hi, odd_lo)

            @pl.when(at == 0)
            def _():
                part_cos[where_to, :] = new_cos
                part_sin[where_to, :] = new_sin

            @pl.when(at > 0)
            def _():
                part_cos[where_to, :] += new_cos
                part_sin[where_to, :] += new_sin

            return carry

        lax.fori_loop(0, part_cos.shape[0] // tall, one_group, 0)

    @pl.when(step == pl.num_programs(0) - 1)
    def _():
        tall = 64
        owner = lax.broadcasted_iota(jnp.int32, (tall, 128), 1) // lat_here

        def fold(g, carry):
            where_from = pl.ds(pl.multiple_of(g * tall, tall), tall)
            even, odd = part_cos[where_from, :], part_sin[where_from, :]
            for side, full in enumerate((even + odd, even - odd)):
                chosen = None
                for n in range(2 * members):
                    piece = full[:, n * 128:(n + 1) * 128]
                    if n >= members:
                        piece = jnp.abs(piece)
                    reach = lat_here
                    while reach < 128:
                        piece = jnp.maximum(piece, pltpu.roll(piece, reach, 1))
                        reach *= 2
                    chosen = piece if chosen is None else jnp.where(owner == n, piece, chosen)
                out_ref[side, where_from, :] = chosen
            return carry

        lax.fori_loop(0, part_cos.shape[0] // tall, fold, 0)

        def drain(chunk, carry):
            for ahead in range(1, narrow):
                copy_to(chunk, ahead).wait_send()
            return carry

        lax.fori_loop(0, chunks, drain, 0)


def region_kernel(regions, edge_ref, field_ref, out_ref):
    half = field_ref.shape[1]
    row = lax.broadcasted_iota(jnp.int32, (WINDOW, 128), 0)

    def one_region(r, carry):
        begin, end = edge_ref[r], edge_ref[r + 1]
        best = jnp.full((1, 128), -1e30, jnp.float32)
        for side in range(2):
            low = half - end if side == 0 else begin - half
            high = half - begin if side == 0 else end - half
            at = jnp.clip(low // 8 * 8, 0, half - WINDOW)
            at = pl.multiple_of(at, 8)
            data = field_ref[side, pl.ds(at, WINDOW), :]
            here = (row >= low - at) & (row < high - at)
            best = jnp.maximum(best, jnp.max(jnp.where(here, data, -1e30), axis=0, keepdims=True))
        out_ref[pl.ds(r, 1), :] = best
        return carry

    lax.fori_loop(0, regions, one_region, 0)


def wide_kernel(wide, mine_ref, out_ref, held, send_sem, recv_sem):
    me = lax.axis_index("wide")
    count = out_ref.shape[0]
    greet("wide", wide)

    def copy(ahead, arriving):
        other = lax.rem(me + ahead, wide)
        return pltpu.make_async_remote_copy(
            src_ref=mine_ref.at[other], dst_ref=held.at[other if arriving else me],
            send_sem=send_sem.at[other], recv_sem=recv_sem.at[other if arriving else me],
            device_id={"wide": other}, device_id_type=MESH,
        )

    for ahead in range(1, wide):
        copy(ahead, False).start()
    best = mine_ref[me]
    for ahead in range(1, wide):
        copy(ahead, True).wait_recv()
        best = jnp.maximum(best, held[lax.rem(me + ahead, wide)])
    out_ref[...] = best
    for ahead in range(1, wide):
        copy(ahead, False).wait_send()


def per_device(spectra, legendre, pair_of_slot, lat_owner, region_of_lon):
    members, steps_here, slot_count, _, length = spectra.shape
    half_count = legendre.shape[0]
    lat = legendre.shape[2]
    narrow, wide = lax.axis_size("narrow"), lax.axis_size("wide")
    lat_here = lat // narrow
    lon = region_of_lon.shape[0]
    half_lon = lon // 2
    rows = members * steps_here * 2
    chunks = slot_count // CHUNK
    here = lax.axis_index("narrow")
    paired = lax.dynamic_slice_in_dim(pair_of_slot, here * slot_count, slot_count)

    ids = jnp.arange(lat, dtype=jnp.int32)
    before = (lat_owner[:, None] < lat_owner[None, :]) | (
        (lat_owner[:, None] == lat_owner[None, :]) & (ids[:, None] < ids[None, :])
    )
    rank = jnp.sum(before.astype(jnp.int32), axis=0)
    rank = jnp.concatenate([rank[:lat // 2], jnp.flip(rank[lat // 2:])])
    target = (rank // lat_here)[None, :] * 128 + jnp.arange(steps_here)[:, None] * lat_here + (rank % lat_here)[None, :]
    place = (target.reshape(-1)[:, None] == jnp.arange(narrow * 128)[None, :]).astype(jnp.bfloat16)

    lead = jnp.transpose(pair_of_slot.reshape(narrow, chunks, CHUNK), (1, 0, 2))
    waves = jnp.stack([lead, M - 1 - lead], axis=2).reshape(-1)
    unit = 2.0 * math.pi / (2 * LON_FULL)

    def angle(factor):
        return ((waves * factor) % (2 * LON_FULL)).astype(jnp.float32) * unit

    start = angle(lon - 1)
    scale = M ** -0.5
    turn = jnp.stack(
        [jnp.cos(start) * scale, jnp.sin(start) * scale, waves.astype(jnp.float32) / M, jnp.zeros_like(start)], axis=1
    )
    coarse = angle((jnp.arange(half_lon // FINE, dtype=jnp.int32) * (2 * FINE))[:, None])
    fine = angle((jnp.arange(FINE, dtype=jnp.int32) * 2 + 1)[:, None])
    coarse = jnp.stack([jnp.cos(coarse), jnp.sin(coarse)])
    fine = jnp.stack([jnp.cos(fine), jnp.sin(fine)])

    dims = (narrow, chunks, rows, members, steps_here, lat_here)
    depth = KCHUNKS * narrow * 2 * CHUNK
    lanes = 2 * members * 128
    tail = chunks // KCHUNKS

    def first(i, *_):
        return jnp.minimum(i, chunks - 1)

    def later(i, *_):
        return jnp.maximum(i - chunks, 0)

    fields = pl.pallas_call(
        functools.partial(fields_kernel, dims),
        grid=(chunks + tail,),
        in_specs=[
            pl.BlockSpec(memory_space=pltpu.SMEM),
            pl.BlockSpec((members, steps_here, CHUNK, 2, length), lambda i: (0, 0, first(i), 0, 0)),
            pl.BlockSpec((length, CHUNK // 2, lat), lambda i: (0, first(i), 0)),
            pl.BlockSpec(place.shape, lambda i: (0, 0)),
            pl.BlockSpec((depth, turn.shape[1]), lambda i: (later(i), 0)),
            pl.BlockSpec((2, half_lon // FINE, depth), lambda i: (0, 0, later(i))),
            pl.BlockSpec((2, FINE, depth), lambda i: (0, 0, later(i))),
        ],
        out_specs=pl.BlockSpec((2, half_lon, 128), lambda i: (0, 0, 0)),
        out_shape=jax.ShapeDtypeStruct((2, half_lon, 128), jnp.float32),
        scratch_shapes=[
            pltpu.VMEM((2, rows, length), jnp.float32),
            pltpu.VMEM((length * CHUNK // 2, 128), jnp.float32),
            pltpu.VMEM((2 * CHUNK * rows, 128), jnp.float32),
            pltpu.VMEM((chunks, narrow, 2 * CHUNK, lanes), jnp.float32),
            pltpu.VMEM((chunks, narrow, 2 * CHUNK, lanes), jnp.float32),
            pltpu.VMEM((half_lon, lanes), jnp.float32),
            pltpu.VMEM((half_lon, lanes), jnp.float32),
            pltpu.SemaphoreType.DMA((chunks, narrow)),
            pltpu.SemaphoreType.DMA((chunks, narrow)),
        ],
        compiler_params=pltpu.CompilerParams(
            collective_id=0, has_side_effects=True, vmem_limit_bytes=56 * 1024 * 1024,
            dimension_semantics=("arbitrary",),
        ),
    )(paired, spectra, jnp.transpose(legendre, (1, 0, 2)), place, turn, coarse, fine)

    regions = REG_DEV * wide
    edges = jnp.sum(
        (region_of_lon[None, :] < jnp.arange(regions + 1, dtype=jnp.int32)[:, None]).astype(jnp.int32), axis=1
    )
    peaks = pl.pallas_call(
        functools.partial(region_kernel, regions),
        in_specs=[pl.BlockSpec(memory_space=pltpu.SMEM), pl.BlockSpec(memory_space=pltpu.VMEM)],
        out_specs=pl.BlockSpec(memory_space=pltpu.VMEM),
        out_shape=jax.ShapeDtypeStruct((regions, 128), jnp.float32),
    )(edges, fields)
    best = pl.pallas_call(
        functools.partial(wide_kernel, wide),
        in_specs=[pl.BlockSpec(memory_space=pltpu.VMEM)],
        out_specs=pl.BlockSpec(memory_space=pltpu.VMEM),
        out_shape=jax.ShapeDtypeStruct((REG_DEV, 128), jnp.float32),
        scratch_shapes=[
            pltpu.VMEM((wide, REG_DEV, 128), jnp.float32),
            pltpu.SemaphoreType.DMA((wide,)),
            pltpu.SemaphoreType.DMA((wide,)),
        ],
        compiler_params=pltpu.CompilerParams(collective_id=1, has_side_effects=True),
    )(peaks.reshape(wide, REG_DEV, 128))
    best = jnp.transpose(best.reshape(REG_DEV, 2, members, lat_here), (1, 2, 3, 0))
    return (best[0], best[1])


def solution(mesh):
    in_specs = (
        P(None, ("groups", "wide"), "narrow", None, None),
        P("narrow", None, None),
        P(),
        P(),
        P(),
    )
    out_specs = (P("groups", "narrow", "wide"), P("groups", "narrow", "wide"))

    def body(spectra, legendre, *rest):
        members, steps_here, slot_count = spectra.shape[:3]
        lat_here = legendre.shape[2] // mesh.shape["narrow"]
        packs = steps_here * lat_here == 128 and 2 * members * lat_here == 128
        packs = packs and slot_count % (CHUNK * KCHUNKS) == 0 and legendre.shape[2] == 128
        chosen = per_device if packs else per_device_plain
        return chosen(spectra, legendre, *rest)

    return jax.shard_map(
        body, mesh=mesh, in_specs=in_specs, out_specs=out_specs, check_vma=False
    )
```

```python
import functools
import math

import jax
import jax.numpy as jnp
from jax import lax
from jax.experimental import pallas as pl
from jax.experimental.pallas import tpu as pltpu
from jax.sharding import PartitionSpec as P

M = 1280
LON = 2048
REG_DEV = 16
LON_FULL = 5120


def synthesize(operand, waves, start, width):
    columns = start + jnp.arange(width, dtype=jnp.int32)
    phase = waves[:, None] * columns[None, :] % LON_FULL
    angle = phase.astype(jnp.float32) * (2.0 * math.pi / LON_FULL)
    cosine = jnp.cos(angle)
    sine = jnp.sin(angle)
    rate = (waves.astype(jnp.float32) / M)[:, None]
    upper = jnp.concatenate([cosine, -rate * sine], axis=1)
    lower = jnp.concatenate([-sine, -rate * cosine], axis=1)
    table = jnp.concatenate([upper, lower], axis=0) * M ** (-0.5)
    return jnp.dot(operand, table, precision=lax.Precision.HIGHEST)


def synthesize_all(operand, waves):
    width = min(512, LON)
    starts = jnp.arange(LON // width, dtype=jnp.int32) * width

    def one_block(begin):
        return synthesize(operand, waves, begin, width)

    blocks = lax.map(one_block, starts)
    blocks = blocks.reshape(blocks.shape[0], blocks.shape[1], 2, width)
    value = jnp.transpose(blocks[:, :, 0], (1, 0, 2)).reshape(operand.shape[0], LON)
    slope = jnp.transpose(blocks[:, :, 1], (1, 0, 2)).reshape(operand.shape[0], LON)
    return (value, slope)


def region_peak(values, region_of_lon, wanted):
    hits = region_of_lon[:, None] == wanted[None, :]
    masked = jnp.where(hits[None, None], values[..., None], -1e30)
    return masked.max(axis=2)


def per_device_plain(spectra, legendre, pair_of_slot, lat_owner, region_of_lon):
    members = spectra.shape[0]
    steps_here = spectra.shape[1]
    slot_count = spectra.shape[2]
    length = spectra.shape[4]
    half_count = legendre.shape[0]
    lat_half = legendre.shape[2] // 2
    here = lax.axis_index("narrow")
    paired = lax.dynamic_slice_in_dim(pair_of_slot, here * slot_count, slot_count)
    position = jnp.arange(length, dtype=jnp.int32)[None, :]
    first_len = (M - paired)[:, None]
    leading = position < first_len
    offset = jnp.where(leading, position, position - first_len)
    even_term = offset % 2 == 0
    masks = jnp.stack(
        [leading & even_term, leading & ~even_term, ~leading & even_term, ~leading & ~even_term],
        axis=1,
    ).astype(jnp.bfloat16)
    ordered = jnp.transpose(spectra, (2, 0, 1, 3, 4))
    masked = masks[:, :, None, None, None, :] * ordered[:, None]
    masked = masked.reshape(half_count, 2, -1, length)
    table = legendre.reshape(half_count, length, 2, lat_half)
    sums = jnp.einsum("abrl,albj->abrj", masked, table, preferred_element_type=jnp.float32)
    sums = sums.reshape(slot_count, 4, members, steps_here, 2, lat_half)
    north_lead = sums[:, 0] + sums[:, 1]
    south_lead = sums[:, 0] - sums[:, 1]
    north_tail = sums[:, 2] + sums[:, 3]
    south_tail = sums[:, 2] - sums[:, 3]
    lead = jnp.concatenate([north_lead, jnp.flip(south_lead, axis=-1)], axis=-1)
    tail = jnp.concatenate([north_tail, jnp.flip(south_tail, axis=-1)], axis=-1)
    waved = jnp.stack([lead, tail], axis=1).reshape(2 * slot_count, members, steps_here, 2, -1)
    order = jnp.argsort(lat_owner, stable=True)
    waved = jnp.take(waved, order, axis=4)
    arrived = lax.all_to_all(waved, "narrow", split_axis=4, concat_axis=0, tiled=True)
    waves = jnp.stack([pair_of_slot, M - 1 - pair_of_slot], axis=1).reshape(-1)
    lat_here = arrived.shape[4]
    operand = jnp.transpose(arrived, (1, 2, 4, 3, 0)).reshape(members * steps_here * lat_here, -1)
    value, slope = synthesize_all(operand, waves)
    value = value.reshape(members, steps_here, lat_here, LON).max(axis=1)
    slope = jnp.abs(slope).reshape(members, steps_here, lat_here, LON).max(axis=1)
    wide_count = lax.axis_size("wide")
    mine_start = lax.axis_index("wide") * REG_DEV
    wanted = jnp.arange(REG_DEV * wide_count, dtype=jnp.int32)
    peaks = region_peak(value, region_of_lon, wanted)
    slopes = region_peak(slope, region_of_lon, wanted)
    peaks, slopes = lax.pmax((peaks, slopes), "wide")
    peak = lax.dynamic_slice_in_dim(peaks, mine_start, REG_DEV, 2)
    peak_slope = lax.dynamic_slice_in_dim(slopes, mine_start, REG_DEV, 2)
    return (peak, peak_slope)


CHUNK = 16
KCHUNKS = 2
UNROLL = 2
FINE = 32
WINDOW = 56
MESH = pl.DeviceIdType.MESH


def greet(axis, count):
    me = lax.axis_index(axis)
    barrier = pltpu.get_barrier_semaphore()
    for step in range(1, count):
        pl.semaphore_signal(barrier, inc=1, device_id={axis: lax.rem(me + step, count)}, device_id_type=MESH)
    pl.semaphore_wait(barrier, count - 1)


def split(values):
    high = values.astype(jnp.bfloat16)
    low = (values - high.astype(jnp.float32)).astype(jnp.bfloat16)
    return high, low


def dot(left, right):
    return jnp.dot(left, right, preferred_element_type=jnp.float32)


def fields_kernel(
    dims, first_ref, x_ref, table_ref, place_ref, turn_ref, coarse_ref, fine_ref, out_ref,
    lined, spread, sums, sent, held, part_cos, part_sin, send_sem, recv_sem,
):
    narrow, chunks, rows, members, steps_here, lat_here = dims
    step = pl.program_id(0)
    me = lax.axis_index("narrow")
    lanes = members * 2 * 128

    def copy_to(chunk, ahead):
        target = lax.rem(me + ahead, narrow)
        return pltpu.make_async_remote_copy(
            src_ref=sent.at[chunk, target], dst_ref=held.at[chunk, me],
            send_sem=send_sem.at[chunk, target], recv_sem=recv_sem.at[chunk, me],
            device_id={"narrow": target}, device_id_type=MESH,
        )

    def copy_from(chunk, ahead):
        origin = lax.rem(me + ahead, narrow)
        return pltpu.make_async_remote_copy(
            src_ref=sent.at[chunk, origin], dst_ref=held.at[chunk, origin],
            send_sem=send_sem.at[chunk, origin], recv_sem=recv_sem.at[chunk, origin],
            device_id={"narrow": origin}, device_id_type=MESH,
        )

    @pl.when(step == 0)
    def _():
        greet("narrow", narrow)

    @pl.when((step >= 1) & (step <= chunks))
    def _():
        for ahead in (2, 1, 3) if narrow == 4 else range(1, narrow):
            copy_to(step - 1, ahead).start()

    @pl.when(step < chunks)
    def _():
        position = lax.broadcasted_iota(jnp.int32, (1, M), 1)
        lane = lax.broadcasted_iota(jnp.int32, (rows, 128), 1)
        pairs = CHUNK // 2
        block = M // 8

        def widen(n, carry):
            part = table_ref[pl.ds(n * block, block)].astype(jnp.float32)
            where_to = pl.ds(pl.multiple_of(n * block * pairs, 8), block * pairs)
            spread[where_to, :] = part.reshape(block * pairs, 128)
            return carry

        lax.fori_loop(0, 8, widen, 0)
        spread[M * pairs:, :] = table_ref[M].astype(jnp.float32)

        def one_pair(at, lines):
            parts = []
            extras = []
            for half in range(2):
                slot = 2 * at + half
                first_len = M - first_ref[step * CHUNK + slot]
                leading = (position < first_len).astype(jnp.float32)
                trailing = 1.0 - leading
                sign_lead = (1 - 2 * (position & 1)).astype(jnp.float32)
                flip = (1 - 2 * (first_len & 1)).astype(jnp.float32)
                for e in range(members):
                    for t in range(steps_here):
                        row = 2 * (e * steps_here + t)
                        lined[lines + half, row:row + 2, :] = x_ref[e, t, slot].astype(jnp.float32)
                body = lined[lines + half, :, :M].astype(jnp.bfloat16)
                for mask in (leading, leading * sign_lead, trailing, trailing * (sign_lead * flip)):
                    parts.append(body * mask.astype(jnp.bfloat16))
                last = lined[lines + half, :, M:]
                extras.append((last, flip))
            table = spread[pl.ds(at, M, stride=pairs), :].astype(jnp.bfloat16)
            out = dot(jnp.concatenate(parts, axis=0), table)
            edge = spread[pl.ds(M * pairs + at, 1), :]
            for half in range(2):
                base = half * 4 * rows
                piece = [out[base + v * rows:base + (v + 1) * rows] for v in range(4)]
                last, flip = extras[half]
                term = last * edge
                piece[2] = piece[2] + term
                piece[3] = piece[3] + term * flip
                for tail_at in range(2):
                    north, south = piece[2 * tail_at], piece[2 * tail_at + 1]
                    if half == 0:
                        both = jnp.where(lane < 64, north, pltpu.roll(south, 64, 1))
                    else:
                        both = jnp.where(lane < 64, pltpu.roll(north, 64, 1), south)
                    at_row = (tail_at * CHUNK + 2 * at + half) * rows
                    sums[pl.ds(pl.multiple_of(at_row, rows), rows), :] = both

        def some_pairs(n, carry):
            for u in range(UNROLL):
                one_pair(n * UNROLL + u, 2 * u)
            return carry

        lax.fori_loop(0, CHUNK // 2 // UNROLL, some_pairs, 0)
        highs, lows = [], []
        for c in range(2):
            for e in range(members):
                wide_rows = jnp.concatenate(
                    [sums[pl.ds((e * steps_here + t) * 2 + c, 2 * CHUNK, stride=rows), :] for t in range(steps_here)],
                    axis=1,
                )
                high, low = split(wide_rows)
                highs.append(high)
                lows.append(low)
        both = dot(jnp.concatenate(highs + lows, axis=0), place_ref[...])
        count = 2 * members * 2 * CHUNK
        moved = both[:count] + both[count:]
        for n in range(2 * members):
            for d in range(narrow):
                sent[step, d, :, n * 128:(n + 1) * 128] = (
                    moved[n * 2 * CHUNK:(n + 1) * 2 * CHUNK, d * 128:(d + 1) * 128]
                )
        held[step, me] = sent[step, me]

    @pl.when(step >= chunks)
    def _():
        at = step - chunks
        half = members * 128
        for k in range(KCHUNKS):
            for ahead in range(1, narrow):
                copy_from(at * KCHUNKS + k, ahead).wait_recv()
        depth = KCHUNKS * narrow * 2 * CHUNK
        data = jnp.concatenate(
            [held[at * KCHUNKS + k, d] for k in range(KCHUNKS) for d in range(narrow)], axis=0
        )
        real, imag = data[:, :half], data[:, half:]
        turn = turn_ref[...]
        cos0, sin0, rate = turn[:, 0:1], turn[:, 1:2], turn[:, 2:3]
        a = real * cos0 - imag * sin0
        b = real * sin0 + imag * cos0
        even_hi, even_lo = split(jnp.concatenate([a, -rate * b], axis=1))
        odd_hi, odd_lo = split(jnp.concatenate([b, rate * a], axis=1))
        group = 8
        tall = group * FINE

        def one_group(g, carry):
            cosines, sines = [], []
            c2, s2 = fine_ref[0], fine_ref[1]
            cu = coarse_ref[0, pl.ds(pl.multiple_of(g * group, group), group), :]
            su = coarse_ref[1, pl.ds(pl.multiple_of(g * group, group), group), :]
            for u in range(group):
                c1, s1 = cu[u:u + 1], su[u:u + 1]
                cosines.append(c1 * c2 - s1 * s2)
                sines.append(s1 * c2 + c1 * s2)
            cos_hi, cos_lo = split(jnp.concatenate(cosines, axis=0))
            sin_hi, sin_lo = split(jnp.concatenate(sines, axis=0))
            where_to = pl.ds(pl.multiple_of(g * tall, tall), tall)
            new_cos = dot(cos_hi, even_hi) + dot(cos_lo, even_hi) + dot(cos_hi, even_lo)
            new_sin = dot(sin_hi, odd_hi) + dot(sin_lo, odd_hi) + dot(sin_hi, odd_lo)

            @pl.when(at == 0)
            def _():
                part_cos[where_to, :] = new_cos
                part_sin[where_to, :] = new_sin

            @pl.when(at > 0)
            def _():
                part_cos[where_to, :] += new_cos
                part_sin[where_to, :] += new_sin

            return carry

        lax.fori_loop(0, part_cos.shape[0] // tall, one_group, 0)

    @pl.when(step == pl.num_programs(0) - 1)
    def _():
        tall = 64
        owner = lax.broadcasted_iota(jnp.int32, (tall, 128), 1) // lat_here

        def fold(g, carry):
            where_from = pl.ds(pl.multiple_of(g * tall, tall), tall)
            even, odd = part_cos[where_from, :], part_sin[where_from, :]
            for side, full in enumerate((even + odd, even - odd)):
                chosen = None
                for n in range(2 * members):
                    piece = full[:, n * 128:(n + 1) * 128]
                    if n >= members:
                        piece = jnp.abs(piece)
                    reach = lat_here
                    while reach < 128:
                        piece = jnp.maximum(piece, pltpu.roll(piece, reach, 1))
                        reach *= 2
                    chosen = piece if chosen is None else jnp.where(owner == n, piece, chosen)
                out_ref[side, where_from, :] = chosen
            return carry

        lax.fori_loop(0, part_cos.shape[0] // tall, fold, 0)

        def drain(chunk, carry):
            for ahead in range(1, narrow):
                copy_to(chunk, ahead).wait_send()
            return carry

        lax.fori_loop(0, chunks, drain, 0)


def region_kernel(regions, edge_ref, field_ref, out_ref):
    half = field_ref.shape[1]
    row = lax.broadcasted_iota(jnp.int32, (WINDOW, 128), 0)

    def one_region(r, carry):
        begin, end = edge_ref[r], edge_ref[r + 1]
        best = jnp.full((1, 128), -1e30, jnp.float32)
        for side in range(2):
            low = half - end if side == 0 else begin - half
            high = half - begin if side == 0 else end - half
            at = jnp.clip(low // 8 * 8, 0, half - WINDOW)
            at = pl.multiple_of(at, 8)
            data = field_ref[side, pl.ds(at, WINDOW), :]
            here = (row >= low - at) & (row < high - at)
            best = jnp.maximum(best, jnp.max(jnp.where(here, data, -1e30), axis=0, keepdims=True))
        out_ref[pl.ds(r, 1), :] = best
        return carry

    lax.fori_loop(0, regions, one_region, 0)


def wide_kernel(wide, mine_ref, out_ref, held, send_sem, recv_sem):
    me = lax.axis_index("wide")
    count = out_ref.shape[0]
    greet("wide", wide)

    def copy(ahead, arriving):
        other = lax.rem(me + ahead, wide)
        return pltpu.make_async_remote_copy(
            src_ref=mine_ref.at[other], dst_ref=held.at[other if arriving else me],
            send_sem=send_sem.at[other], recv_sem=recv_sem.at[other if arriving else me],
            device_id={"wide": other}, device_id_type=MESH,
        )

    for ahead in range(1, wide):
        copy(ahead, False).start()
    best = mine_ref[me]
    for ahead in range(1, wide):
        copy(ahead, True).wait_recv()
        best = jnp.maximum(best, held[lax.rem(me + ahead, wide)])
    out_ref[...] = best
    for ahead in range(1, wide):
        copy(ahead, False).wait_send()


def per_device(spectra, legendre, pair_of_slot, lat_owner, region_of_lon):
    members, steps_here, slot_count, _, length = spectra.shape
    half_count = legendre.shape[0]
    lat = legendre.shape[2]
    narrow, wide = lax.axis_size("narrow"), lax.axis_size("wide")
    lat_here = lat // narrow
    lon = region_of_lon.shape[0]
    half_lon = lon // 2
    rows = members * steps_here * 2
    chunks = slot_count // CHUNK
    here = lax.axis_index("narrow")
    paired = lax.dynamic_slice_in_dim(pair_of_slot, here * slot_count, slot_count)

    ids = jnp.arange(lat, dtype=jnp.int32)
    before = (lat_owner[:, None] < lat_owner[None, :]) | (
        (lat_owner[:, None] == lat_owner[None, :]) & (ids[:, None] < ids[None, :])
    )
    rank = jnp.sum(before.astype(jnp.int32), axis=0)
    rank = jnp.concatenate([rank[:lat // 2], jnp.flip(rank[lat // 2:])])
    target = (rank // lat_here)[None, :] * 128 + jnp.arange(steps_here)[:, None] * lat_here + (rank % lat_here)[None, :]
    place = (target.reshape(-1)[:, None] == jnp.arange(narrow * 128)[None, :]).astype(jnp.bfloat16)

    lead = jnp.transpose(pair_of_slot.reshape(narrow, chunks, CHUNK), (1, 0, 2))
    waves = jnp.stack([lead, M - 1 - lead], axis=2).reshape(-1)
    unit = 2.0 * math.pi / (2 * LON_FULL)

    def angle(factor):
        return ((waves * factor) % (2 * LON_FULL)).astype(jnp.float32) * unit

    start = angle(lon - 1)
    scale = M ** -0.5
    turn = jnp.stack(
        [jnp.cos(start) * scale, jnp.sin(start) * scale, waves.astype(jnp.float32) / M, jnp.zeros_like(start)], axis=1
    )
    coarse = angle((jnp.arange(half_lon // FINE, dtype=jnp.int32) * (2 * FINE))[:, None])
    fine = angle((jnp.arange(FINE, dtype=jnp.int32) * 2 + 1)[:, None])
    coarse = jnp.stack([jnp.cos(coarse), jnp.sin(coarse)])
    fine = jnp.stack([jnp.cos(fine), jnp.sin(fine)])

    dims = (narrow, chunks, rows, members, steps_here, lat_here)
    depth = KCHUNKS * narrow * 2 * CHUNK
    lanes = 2 * members * 128
    tail = chunks // KCHUNKS

    def first(i, *_):
        return jnp.minimum(i, chunks - 1)

    def later(i, *_):
        return jnp.maximum(i - chunks, 0)

    fields = pl.pallas_call(
        functools.partial(fields_kernel, dims),
        grid=(chunks + tail,),
        in_specs=[
            pl.BlockSpec(memory_space=pltpu.SMEM),
            pl.BlockSpec((members, steps_here, CHUNK, 2, length), lambda i: (0, 0, first(i), 0, 0)),
            pl.BlockSpec((length, CHUNK // 2, lat), lambda i: (0, first(i), 0)),
            pl.BlockSpec(place.shape, lambda i: (0, 0)),
            pl.BlockSpec((depth, turn.shape[1]), lambda i: (later(i), 0)),
            pl.BlockSpec((2, half_lon // FINE, depth), lambda i: (0, 0, later(i))),
            pl.BlockSpec((2, FINE, depth), lambda i: (0, 0, later(i))),
        ],
        out_specs=pl.BlockSpec((2, half_lon, 128), lambda i: (0, 0, 0)),
        out_shape=jax.ShapeDtypeStruct((2, half_lon, 128), jnp.float32),
        scratch_shapes=[
            pltpu.VMEM((2 * UNROLL, rows, length), jnp.float32),
            pltpu.VMEM((length * CHUNK // 2, 128), jnp.float32),
            pltpu.VMEM((2 * CHUNK * rows, 128), jnp.float32),
            pltpu.VMEM((chunks, narrow, 2 * CHUNK, lanes), jnp.float32),
            pltpu.VMEM((chunks, narrow, 2 * CHUNK, lanes), jnp.float32),
            pltpu.VMEM((half_lon, lanes), jnp.float32),
            pltpu.VMEM((half_lon, lanes), jnp.float32),
            pltpu.SemaphoreType.DMA((chunks, narrow)),
            pltpu.SemaphoreType.DMA((chunks, narrow)),
        ],
        compiler_params=pltpu.CompilerParams(
            collective_id=0, has_side_effects=True, vmem_limit_bytes=56 * 1024 * 1024,
            dimension_semantics=("arbitrary",),
        ),
    )(paired, spectra, jnp.transpose(legendre, (1, 0, 2)), place, turn, coarse, fine)

    regions = REG_DEV * wide
    edges = jnp.sum(
        (region_of_lon[None, :] < jnp.arange(regions + 1, dtype=jnp.int32)[:, None]).astype(jnp.int32), axis=1
    )
    peaks = pl.pallas_call(
        functools.partial(region_kernel, regions),
        in_specs=[pl.BlockSpec(memory_space=pltpu.SMEM), pl.BlockSpec(memory_space=pltpu.VMEM)],
        out_specs=pl.BlockSpec(memory_space=pltpu.VMEM),
        out_shape=jax.ShapeDtypeStruct((regions, 128), jnp.float32),
    )(edges, fields)
    best = pl.pallas_call(
        functools.partial(wide_kernel, wide),
        in_specs=[pl.BlockSpec(memory_space=pltpu.VMEM)],
        out_specs=pl.BlockSpec(memory_space=pltpu.VMEM),
        out_shape=jax.ShapeDtypeStruct((REG_DEV, 128), jnp.float32),
        scratch_shapes=[
            pltpu.VMEM((wide, REG_DEV, 128), jnp.float32),
            pltpu.SemaphoreType.DMA((wide,)),
            pltpu.SemaphoreType.DMA((wide,)),
        ],
        compiler_params=pltpu.CompilerParams(collective_id=1, has_side_effects=True),
    )(peaks.reshape(wide, REG_DEV, 128))
    best = jnp.transpose(best.reshape(REG_DEV, 2, members, lat_here), (1, 2, 3, 0))
    return (best[0], best[1])


def solution(mesh):
    in_specs = (
        P(None, ("groups", "wide"), "narrow", None, None),
        P("narrow", None, None),
        P(),
        P(),
        P(),
    )
    out_specs = (P("groups", "narrow", "wide"), P("groups", "narrow", "wide"))

    def body(spectra, legendre, *rest):
        members, steps_here, slot_count = spectra.shape[:3]
        lat_here = legendre.shape[2] // mesh.shape["narrow"]
        packs = steps_here * lat_here == 128 and 2 * members * lat_here == 128
        packs = packs and slot_count % (CHUNK * KCHUNKS) == 0 and legendre.shape[2] == 128
        chosen = per_device if packs else per_device_plain
        return chosen(spectra, legendre, *rest)

    return jax.shard_map(
        body, mesh=mesh, in_specs=in_specs, out_specs=out_specs, check_vma=False
    )
```

```python
import functools
import math

import jax
import jax.numpy as jnp
from jax import lax
from jax.experimental import pallas as pl
from jax.experimental.pallas import tpu as pltpu
from jax.sharding import PartitionSpec as P

M = 1280
LON = 2048
REG_DEV = 16
LON_FULL = 5120


def synthesize(operand, waves, start, width):
    columns = start + jnp.arange(width, dtype=jnp.int32)
    phase = waves[:, None] * columns[None, :] % LON_FULL
    angle = phase.astype(jnp.float32) * (2.0 * math.pi / LON_FULL)
    cosine = jnp.cos(angle)
    sine = jnp.sin(angle)
    rate = (waves.astype(jnp.float32) / M)[:, None]
    upper = jnp.concatenate([cosine, -rate * sine], axis=1)
    lower = jnp.concatenate([-sine, -rate * cosine], axis=1)
    table = jnp.concatenate([upper, lower], axis=0) * M ** (-0.5)
    return jnp.dot(operand, table, precision=lax.Precision.HIGHEST)


def synthesize_all(operand, waves):
    width = min(512, LON)
    starts = jnp.arange(LON // width, dtype=jnp.int32) * width

    def one_block(begin):
        return synthesize(operand, waves, begin, width)

    blocks = lax.map(one_block, starts)
    blocks = blocks.reshape(blocks.shape[0], blocks.shape[1], 2, width)
    value = jnp.transpose(blocks[:, :, 0], (1, 0, 2)).reshape(operand.shape[0], LON)
    slope = jnp.transpose(blocks[:, :, 1], (1, 0, 2)).reshape(operand.shape[0], LON)
    return (value, slope)


def region_peak(values, region_of_lon, wanted):
    hits = region_of_lon[:, None] == wanted[None, :]
    masked = jnp.where(hits[None, None], values[..., None], -1e30)
    return masked.max(axis=2)


def per_device_plain(spectra, legendre, pair_of_slot, lat_owner, region_of_lon):
    members = spectra.shape[0]
    steps_here = spectra.shape[1]
    slot_count = spectra.shape[2]
    length = spectra.shape[4]
    half_count = legendre.shape[0]
    lat_half = legendre.shape[2] // 2
    here = lax.axis_index("narrow")
    paired = lax.dynamic_slice_in_dim(pair_of_slot, here * slot_count, slot_count)
    position = jnp.arange(length, dtype=jnp.int32)[None, :]
    first_len = (M - paired)[:, None]
    leading = position < first_len
    offset = jnp.where(leading, position, position - first_len)
    even_term = offset % 2 == 0
    masks = jnp.stack(
        [leading & even_term, leading & ~even_term, ~leading & even_term, ~leading & ~even_term],
        axis=1,
    ).astype(jnp.bfloat16)
    ordered = jnp.transpose(spectra, (2, 0, 1, 3, 4))
    masked = masks[:, :, None, None, None, :] * ordered[:, None]
    masked = masked.reshape(half_count, 2, -1, length)
    table = legendre.reshape(half_count, length, 2, lat_half)
    sums = jnp.einsum("abrl,albj->abrj", masked, table, preferred_element_type=jnp.float32)
    sums = sums.reshape(slot_count, 4, members, steps_here, 2, lat_half)
    north_lead = sums[:, 0] + sums[:, 1]
    south_lead = sums[:, 0] - sums[:, 1]
    north_tail = sums[:, 2] + sums[:, 3]
    south_tail = sums[:, 2] - sums[:, 3]
    lead = jnp.concatenate([north_lead, jnp.flip(south_lead, axis=-1)], axis=-1)
    tail = jnp.concatenate([north_tail, jnp.flip(south_tail, axis=-1)], axis=-1)
    waved = jnp.stack([lead, tail], axis=1).reshape(2 * slot_count, members, steps_here, 2, -1)
    order = jnp.argsort(lat_owner, stable=True)
    waved = jnp.take(waved, order, axis=4)
    arrived = lax.all_to_all(waved, "narrow", split_axis=4, concat_axis=0, tiled=True)
    waves = jnp.stack([pair_of_slot, M - 1 - pair_of_slot], axis=1).reshape(-1)
    lat_here = arrived.shape[4]
    operand = jnp.transpose(arrived, (1, 2, 4, 3, 0)).reshape(members * steps_here * lat_here, -1)
    value, slope = synthesize_all(operand, waves)
    value = value.reshape(members, steps_here, lat_here, LON).max(axis=1)
    slope = jnp.abs(slope).reshape(members, steps_here, lat_here, LON).max(axis=1)
    wide_count = lax.axis_size("wide")
    mine_start = lax.axis_index("wide") * REG_DEV
    wanted = jnp.arange(REG_DEV * wide_count, dtype=jnp.int32)
    peaks = region_peak(value, region_of_lon, wanted)
    slopes = region_peak(slope, region_of_lon, wanted)
    peaks, slopes = lax.pmax((peaks, slopes), "wide")
    peak = lax.dynamic_slice_in_dim(peaks, mine_start, REG_DEV, 2)
    peak_slope = lax.dynamic_slice_in_dim(slopes, mine_start, REG_DEV, 2)
    return (peak, peak_slope)


CHUNK = 16
KCHUNKS = 2
UNROLL = 4
FINE = 32
WINDOW = 56
MESH = pl.DeviceIdType.MESH


def greet(axis, count):
    me = lax.axis_index(axis)
    barrier = pltpu.get_barrier_semaphore()
    for step in range(1, count):
        pl.semaphore_signal(barrier, inc=1, device_id={axis: lax.rem(me + step, count)}, device_id_type=MESH)
    pl.semaphore_wait(barrier, count - 1)


def split(values):
    high = values.astype(jnp.bfloat16)
    low = (values - high.astype(jnp.float32)).astype(jnp.bfloat16)
    return high, low


def dot(left, right):
    return jnp.dot(left, right, preferred_element_type=jnp.float32)


def fields_kernel(
    dims, first_ref, x_ref, table_ref, place_ref, turn_ref, coarse_ref, fine_ref, out_ref,
    lined, spread, sums, sent, held, part_cos, part_sin, send_sem, recv_sem,
):
    narrow, chunks, rows, members, steps_here, lat_here = dims
    step = pl.program_id(0)
    me = lax.axis_index("narrow")
    lanes = members * 2 * 128

    def copy_to(chunk, ahead):
        target = lax.rem(me + ahead, narrow)
        return pltpu.make_async_remote_copy(
            src_ref=sent.at[chunk, target], dst_ref=held.at[chunk, me],
            send_sem=send_sem.at[chunk, target], recv_sem=recv_sem.at[chunk, me],
            device_id={"narrow": target}, device_id_type=MESH,
        )

    def copy_from(chunk, ahead):
        origin = lax.rem(me + ahead, narrow)
        return pltpu.make_async_remote_copy(
            src_ref=sent.at[chunk, origin], dst_ref=held.at[chunk, origin],
            send_sem=send_sem.at[chunk, origin], recv_sem=recv_sem.at[chunk, origin],
            device_id={"narrow": origin}, device_id_type=MESH,
        )

    @pl.when(step == 0)
    def _():
        greet("narrow", narrow)

    @pl.when((step >= 1) & (step <= chunks))
    def _():
        for ahead in (2, 1, 3) if narrow == 4 else range(1, narrow):
            copy_to(step - 1, ahead).start()

    @pl.when(step < chunks)
    def _():
        position = lax.broadcasted_iota(jnp.int32, (1, M), 1)
        lane = lax.broadcasted_iota(jnp.int32, (rows, 128), 1)
        pairs = CHUNK // 2
        block = M // 8

        def widen(n, carry):
            part = table_ref[pl.ds(n * block, block)].astype(jnp.float32)
            where_to = pl.ds(pl.multiple_of(n * block * pairs, 8), block * pairs)
            spread[where_to, :] = part.reshape(block * pairs, 128)
            return carry

        lax.fori_loop(0, 8, widen, 0)
        spread[M * pairs:, :] = table_ref[M].astype(jnp.float32)

        def one_pair(at, lines):
            parts = []
            extras = []
            for half in range(2):
                slot = 2 * at + half
                first_len = M - first_ref[(me * chunks + step) * CHUNK + slot]
                leading = (position < first_len).astype(jnp.float32)
                trailing = 1.0 - leading
                sign_lead = (1 - 2 * (position & 1)).astype(jnp.float32)
                flip = (1 - 2 * (first_len & 1)).astype(jnp.float32)
                for e in range(members):
                    for t in range(steps_here):
                        row = 2 * (e * steps_here + t)
                        lined[lines + half, row:row + 2, :] = x_ref[e, t, slot].astype(jnp.float32)
                body = lined[lines + half, :, :M].astype(jnp.bfloat16)
                for mask in (leading, leading * sign_lead, trailing, trailing * (sign_lead * flip)):
                    parts.append(body * mask.astype(jnp.bfloat16))
                last = lined[lines + half, :, M:]
                extras.append((last, flip))
            table = spread[pl.ds(at, M, stride=pairs), :].astype(jnp.bfloat16)
            out = dot(jnp.concatenate(parts, axis=0), table)
            edge = spread[pl.ds(M * pairs + at, 1), :]
            for half in range(2):
                base = half * 4 * rows
                piece = [out[base + v * rows:base + (v + 1) * rows] for v in range(4)]
                last, flip = extras[half]
                term = last * edge
                piece[2] = piece[2] + term
                piece[3] = piece[3] + term * flip
                for tail_at in range(2):
                    north, south = piece[2 * tail_at], piece[2 * tail_at + 1]
                    if half == 0:
                        both = jnp.where(lane < 64, north, pltpu.roll(south, 64, 1))
                    else:
                        both = jnp.where(lane < 64, pltpu.roll(north, 64, 1), south)
                    at_row = (tail_at * CHUNK + 2 * at + half) * rows
                    sums[pl.ds(pl.multiple_of(at_row, rows), rows), :] = both

        def some_pairs(n, carry):
            for u in range(UNROLL):
                one_pair(n * UNROLL + u, 2 * u)
            return carry

        lax.fori_loop(0, CHUNK // 2 // UNROLL, some_pairs, 0)
        highs, lows = [], []
        for c in range(2):
            for e in range(members):
                wide_rows = jnp.concatenate(
                    [sums[pl.ds((e * steps_here + t) * 2 + c, 2 * CHUNK, stride=rows), :] for t in range(steps_here)],
                    axis=1,
                )
                high, low = split(wide_rows)
                highs.append(high)
                lows.append(low)
        both = dot(jnp.concatenate(highs + lows, axis=0), place_ref[...])
        count = 2 * members * 2 * CHUNK
        moved = both[:count] + both[count:]
        for n in range(2 * members):
            for d in range(narrow):
                sent[step, d, :, n * 128:(n + 1) * 128] = (
                    moved[n * 2 * CHUNK:(n + 1) * 2 * CHUNK, d * 128:(d + 1) * 128]
                )
        held[step, me] = sent[step, me]

    @pl.when(step >= chunks)
    def _():
        at = step - chunks
        half = members * 128
        for k in range(KCHUNKS):
            for ahead in range(1, narrow):
                copy_from(at * KCHUNKS + k, ahead).wait_recv()
        depth = KCHUNKS * narrow * 2 * CHUNK
        data = jnp.concatenate(
            [held[at * KCHUNKS + k, d] for k in range(KCHUNKS) for d in range(narrow)], axis=0
        )
        real, imag = data[:, :half], data[:, half:]
        turn = turn_ref[...]
        cos0, sin0, rate = turn[:, 0:1], turn[:, 1:2], turn[:, 2:3]
        a = real * cos0 - imag * sin0
        b = real * sin0 + imag * cos0
        even_hi, even_lo = split(jnp.concatenate([a, -rate * b], axis=1))
        odd_hi, odd_lo = split(jnp.concatenate([b, rate * a], axis=1))
        group = 8
        tall = group * FINE

        def one_group(g, carry):
            cosines, sines = [], []
            c2, s2 = fine_ref[0], fine_ref[1]
            cu = coarse_ref[0, pl.ds(pl.multiple_of(g * group, group), group), :]
            su = coarse_ref[1, pl.ds(pl.multiple_of(g * group, group), group), :]
            for u in range(group):
                c1, s1 = cu[u:u + 1], su[u:u + 1]
                cosines.append(c1 * c2 - s1 * s2)
                sines.append(s1 * c2 + c1 * s2)
            cos_hi, cos_lo = split(jnp.concatenate(cosines, axis=0))
            sin_hi, sin_lo = split(jnp.concatenate(sines, axis=0))
            where_to = pl.ds(pl.multiple_of(g * tall, tall), tall)
            new_cos = dot(cos_hi, even_hi) + dot(cos_lo, even_hi) + dot(cos_hi, even_lo)
            new_sin = dot(sin_hi, odd_hi) + dot(sin_lo, odd_hi) + dot(sin_hi, odd_lo)

            @pl.when(at == 0)
            def _():
                part_cos[where_to, :] = new_cos
                part_sin[where_to, :] = new_sin

            @pl.when(at > 0)
            def _():
                part_cos[where_to, :] += new_cos
                part_sin[where_to, :] += new_sin

            return carry

        lax.fori_loop(0, part_cos.shape[0] // tall, one_group, 0)

    @pl.when(step == pl.num_programs(0) - 1)
    def _():
        tall = 64
        owner = lax.broadcasted_iota(jnp.int32, (tall, 128), 1) // lat_here

        def fold(g, carry):
            where_from = pl.ds(pl.multiple_of(g * tall, tall), tall)
            even, odd = part_cos[where_from, :], part_sin[where_from, :]
            for side, full in enumerate((even + odd, even - odd)):
                chosen = None
                for n in range(2 * members):
                    piece = full[:, n * 128:(n + 1) * 128]
                    if n >= members:
                        piece = jnp.abs(piece)
                    reach = lat_here
                    while reach < 128:
                        piece = jnp.maximum(piece, pltpu.roll(piece, reach, 1))
                        reach *= 2
                    chosen = piece if chosen is None else jnp.where(owner == n, piece, chosen)
                out_ref[side, where_from, :] = chosen
            return carry

        lax.fori_loop(0, part_cos.shape[0] // tall, fold, 0)

        def drain(chunk, carry):
            for ahead in range(1, narrow):
                copy_to(chunk, ahead).wait_send()
            return carry

        lax.fori_loop(0, chunks, drain, 0)


def region_kernel(regions, edge_ref, field_ref, out_ref):
    half = field_ref.shape[1]
    row = lax.broadcasted_iota(jnp.int32, (WINDOW, 128), 0)

    def one_region(r, carry):
        begin, end = edge_ref[r], edge_ref[r + 1]
        best = jnp.full((1, 128), -1e30, jnp.float32)
        for side in range(2):
            low = half - end if side == 0 else begin - half
            high = half - begin if side == 0 else end - half
            at = jnp.clip(low // 8 * 8, 0, half - WINDOW)
            at = pl.multiple_of(at, 8)
            data = field_ref[side, pl.ds(at, WINDOW), :]
            here = (row >= low - at) & (row < high - at)
            best = jnp.maximum(best, jnp.max(jnp.where(here, data, -1e30), axis=0, keepdims=True))
        out_ref[pl.ds(r, 1), :] = best
        return carry

    lax.fori_loop(0, regions, one_region, 0)


def wide_kernel(wide, mine_ref, out_ref, held, send_sem, recv_sem):
    me = lax.axis_index("wide")
    count = out_ref.shape[0]
    greet("wide", wide)

    def copy(ahead, arriving):
        other = lax.rem(me + ahead, wide)
        return pltpu.make_async_remote_copy(
            src_ref=mine_ref.at[other], dst_ref=held.at[other if arriving else me],
            send_sem=send_sem.at[other], recv_sem=recv_sem.at[other if arriving else me],
            device_id={"wide": other}, device_id_type=MESH,
        )

    for ahead in range(1, wide):
        copy(ahead, False).start()
    best = mine_ref[me]
    for ahead in range(1, wide):
        copy(ahead, True).wait_recv()
        best = jnp.maximum(best, held[lax.rem(me + ahead, wide)])
    out_ref[...] = best
    for ahead in range(1, wide):
        copy(ahead, False).wait_send()


def per_device(spectra, legendre, pair_of_slot, lat_owner, region_of_lon):
    members, steps_here, slot_count, _, length = spectra.shape
    half_count = legendre.shape[0]
    lat = legendre.shape[2]
    narrow, wide = lax.axis_size("narrow"), lax.axis_size("wide")
    lat_here = lat // narrow
    lon = region_of_lon.shape[0]
    half_lon = lon // 2
    rows = members * steps_here * 2
    chunks = slot_count // CHUNK

    ids = jnp.arange(lat, dtype=jnp.int32)
    before = (lat_owner[:, None] < lat_owner[None, :]) | (
        (lat_owner[:, None] == lat_owner[None, :]) & (ids[:, None] < ids[None, :])
    )
    rank = jnp.sum(before.astype(jnp.int32), axis=0)
    rank = jnp.concatenate([rank[:lat // 2], jnp.flip(rank[lat // 2:])])
    target = (rank // lat_here)[None, :] * 128 + jnp.arange(steps_here)[:, None] * lat_here + (rank % lat_here)[None, :]
    place = (target.reshape(-1)[:, None] == jnp.arange(narrow * 128)[None, :]).astype(jnp.bfloat16)

    lead = jnp.transpose(pair_of_slot.reshape(narrow, chunks, CHUNK), (1, 0, 2))
    waves = jnp.stack([lead, M - 1 - lead], axis=2).reshape(-1)
    unit = 2.0 * math.pi / (2 * LON_FULL)

    def angle(factor):
        return ((waves * factor) % (2 * LON_FULL)).astype(jnp.float32) * unit

    start = angle(lon - 1)
    scale = M ** -0.5
    turn = jnp.stack(
        [jnp.cos(start) * scale, jnp.sin(start) * scale, waves.astype(jnp.float32) / M, jnp.zeros_like(start)], axis=1
    )
    coarse = angle((jnp.arange(half_lon // FINE, dtype=jnp.int32) * (2 * FINE))[:, None])
    fine = angle((jnp.arange(FINE, dtype=jnp.int32) * 2 + 1)[:, None])
    coarse = jnp.stack([jnp.cos(coarse), jnp.sin(coarse)])
    fine = jnp.stack([jnp.cos(fine), jnp.sin(fine)])

    dims = (narrow, chunks, rows, members, steps_here, lat_here)
    depth = KCHUNKS * narrow * 2 * CHUNK
    lanes = 2 * members * 128
    tail = chunks // KCHUNKS

    def first(i, *_):
        return jnp.minimum(i, chunks - 1)

    def later(i, *_):
        return jnp.maximum(i - chunks, 0)

    fields = pl.pallas_call(
        functools.partial(fields_kernel, dims),
        grid=(chunks + tail,),
        in_specs=[
            pl.BlockSpec(memory_space=pltpu.SMEM),
            pl.BlockSpec((members, steps_here, CHUNK, 2, length), lambda i: (0, 0, first(i), 0, 0)),
            pl.BlockSpec((length, CHUNK // 2, lat), lambda i: (0, first(i), 0)),
            pl.BlockSpec(place.shape, lambda i: (0, 0)),
            pl.BlockSpec((depth, turn.shape[1]), lambda i: (later(i), 0)),
            pl.BlockSpec((2, half_lon // FINE, depth), lambda i: (0, 0, later(i))),
            pl.BlockSpec((2, FINE, depth), lambda i: (0, 0, later(i))),
        ],
        out_specs=pl.BlockSpec((2, half_lon, 128), lambda i: (0, 0, 0)),
        out_shape=jax.ShapeDtypeStruct((2, half_lon, 128), jnp.float32),
        scratch_shapes=[
            pltpu.VMEM((2 * UNROLL, rows, length), jnp.float32),
            pltpu.VMEM((length * CHUNK // 2, 128), jnp.float32),
            pltpu.VMEM((2 * CHUNK * rows, 128), jnp.float32),
            pltpu.VMEM((chunks, narrow, 2 * CHUNK, lanes), jnp.float32),
            pltpu.VMEM((chunks, narrow, 2 * CHUNK, lanes), jnp.float32),
            pltpu.VMEM((half_lon, lanes), jnp.float32),
            pltpu.VMEM((half_lon, lanes), jnp.float32),
            pltpu.SemaphoreType.DMA((chunks, narrow)),
            pltpu.SemaphoreType.DMA((chunks, narrow)),
        ],
        compiler_params=pltpu.CompilerParams(
            collective_id=0, has_side_effects=True, vmem_limit_bytes=56 * 1024 * 1024,
            dimension_semantics=("arbitrary",),
        ),
    )(pair_of_slot, spectra, jnp.transpose(legendre, (1, 0, 2)), place, turn, coarse, fine)

    regions = REG_DEV * wide
    edges = jnp.sum(
        (region_of_lon[None, :] < jnp.arange(regions + 1, dtype=jnp.int32)[:, None]).astype(jnp.int32), axis=1
    )
    peaks = pl.pallas_call(
        functools.partial(region_kernel, regions),
        in_specs=[pl.BlockSpec(memory_space=pltpu.SMEM), pl.BlockSpec(memory_space=pltpu.VMEM)],
        out_specs=pl.BlockSpec(memory_space=pltpu.VMEM),
        out_shape=jax.ShapeDtypeStruct((regions, 128), jnp.float32),
    )(edges, fields)
    best = pl.pallas_call(
        functools.partial(wide_kernel, wide),
        in_specs=[pl.BlockSpec(memory_space=pltpu.VMEM)],
        out_specs=pl.BlockSpec(memory_space=pltpu.VMEM),
        out_shape=jax.ShapeDtypeStruct((REG_DEV, 128), jnp.float32),
        scratch_shapes=[
            pltpu.VMEM((wide, REG_DEV, 128), jnp.float32),
            pltpu.SemaphoreType.DMA((wide,)),
            pltpu.SemaphoreType.DMA((wide,)),
        ],
        compiler_params=pltpu.CompilerParams(collective_id=1, has_side_effects=True),
    )(peaks.reshape(wide, REG_DEV, 128))
    best = jnp.transpose(best.reshape(REG_DEV, 2, members, lat_here), (1, 2, 3, 0))
    return (best[0], best[1])


def solution(mesh):
    in_specs = (
        P(None, ("groups", "wide"), "narrow", None, None),
        P("narrow", None, None),
        P(),
        P(),
        P(),
    )
    out_specs = (P("groups", "narrow", "wide"), P("groups", "narrow", "wide"))

    def body(spectra, legendre, *rest):
        members, steps_here, slot_count = spectra.shape[:3]
        lat_here = legendre.shape[2] // mesh.shape["narrow"]
        packs = steps_here * lat_here == 128 and 2 * members * lat_here == 128
        packs = packs and slot_count % (CHUNK * KCHUNKS) == 0 and legendre.shape[2] == 128
        chosen = per_device if packs else per_device_plain
        return chosen(spectra, legendre, *rest)

    return jax.shard_map(
        body, mesh=mesh, in_specs=in_specs, out_specs=out_specs, check_vma=False
    )
```
